32 devices in a mesh: rep: 4 (over y, core), ep: 8 (over z, x).
Axes of the slice: x: 2, y: 2, z: 4, core: 2. Of those that a mesh axis runs over, the one named last changes fastest.
Arguments:
- tokens: bfloat16 [24576, 2048], P(('rep', 'ep')), may hold values from -6 to 6
- route: int32 [2, 16384], P(None, ('rep', 'ep')), may hold values from 0 to 767, as said below
- cotangent: bfloat16 [2, 16384, 512], P(None, ('rep', 'ep')), may hold values from -6 to 6
- weight: float32 [2, 2048, 512], P(None, 'ep'), may hold values from -0.125 to 0.125
- first_q: int32 [2, 2048, 512], P(None, 'ep'), may hold values from -127 to 127
- first_scale: float32 [2, 2048, 4], P(None, 'ep'), may hold values from 3e-05 to 6e-05
- second_q: int32 [2, 2048, 512], P(None, 'ep'), may hold values from 32 to 127
- second_scale: float32 [2, 2048, 4], P(None, 'ep'), may hold values from 3e-09 to 8e-09
Outputs:
- token_grad: bfloat16 [24576, 2048], P(('rep', 'ep'))
- step_dir: float32 [2, 2048, 512], P(None, 'ep')
- new_weight: float32 [2, 2048, 512], P(None, 'ep')
- next_gate: bfloat16 [2, 16384, 512], P(None, ('rep', 'ep'))
The draws below stay inside these ranges and needn't reach their ends.
Inputs may be any that keep to these rules, and one draw needn't show every extreme that they name: `route`: for each hot expert, the 512 entries of one device's rows (aligned blocks of 512 along the last dimension) are distinct.
All inputs are finite; a program needn't handle non-finite values.
Results may differ from the reference program's by a relative error of at most 0.006.
Values may be sent and summed in bfloat16 or wider, within the bound.
A program may use at most 128 MiB of HBM per device.

```python
import math
import jax
import jax.numpy as jnp
from jax import lax

D = 2048
F = 512
HOT = 2
QBLOCK = 128
ROWS = 512
TOK_DEV = 768
TOKENS = 24576
ALL_ROWS = 16384
N_REP = 4
N_EP = 8


def draw_route(key, part):
    subkeys = jax.random.split(key, HOT * N_REP * N_EP)
    chosen_rows = jax.vmap(lambda one_key: jax.random.permutation(one_key, TOK_DEV)[:ROWS])(subkeys)
    shaped = chosen_rows.reshape(N_REP * N_EP, HOT, ROWS).transpose(1, 0, 2)
    return shaped.reshape(HOT, N_REP * N_EP * ROWS).astype(jnp.int32)


def set_ends(result, key, least, high):
    longest = result.shape.index(max(result.shape))
    spots = []
    for shift in (0, 1):
        where = [jax.random.randint(jax.random.fold_in(key, axis), (), 0, length) for axis, length in enumerate(result.shape)]
        where[longest] = (where[longest] + shift) % result.shape[longest]
        spots.append(tuple(where))
    return result.at[spots[0]].set(least).at[spots[1]].set(high)


def block_levels(rng, extent, cuts, low, largest):
    def one(axis_at, shards_of):
        draws = jax.random.uniform(jax.random.fold_in(jax.random.fold_in(rng, 6), axis_at), (shards_of,), jnp.float32, low / len(cuts), largest / len(cuts))
        return jnp.repeat(jnp.exp(draws), extent[axis_at] // shards_of).reshape((-1,) + (1,) * (len(extent) - axis_at - 1))

    gain = one(*cuts[0])
    for cut in cuts[1:]:
        gain = gain * one(*cut)
    return gain


def noise(key, shape, deviation, bound, cuts=(), held_as=jnp.bfloat16):
    loudness = block_levels(key, shape, cuts, -0.22, 0.18) if cuts else 1.0
    drawn = jax.random.normal(key, shape, jnp.float32) * deviation * loudness
    return jnp.minimum(jnp.maximum(drawn, -bound), bound).astype(held_as)


def setup_inputs(seed: int = 0) -> dict:
    streams_of = jax.random.split(jax.random.key(seed), 9)
    return {
        "tokens": noise(streams_of[0], (TOKENS, D), 1.0, 6.0, ((0, 32),)),
        "route": draw_route(jax.random.fold_in(streams_of[8], 71), 0),
        "cotangent": noise(streams_of[2], (HOT, ALL_ROWS, F), 1.0, 6.0, ((1, 32),)),
        "weight": noise(streams_of[3], (HOT, D, F), D ** -0.5, 0.125, ((1, 8),), jnp.float32),
        "first_q": set_ends(jax.random.randint(streams_of[4], (HOT, D, F), -127, 128), jax.random.fold_in(streams_of[4], 1), -127, 127).astype(jnp.int32),
        "first_scale": jnp.clip(jnp.exp(math.log(5.999999848427251e-05) - 0.6931472 * jax.random.uniform(streams_of[5], (HOT, D, F // QBLOCK), jnp.float32) ** block_levels(streams_of[5], (HOT, D, F // QBLOCK), ((1, 8),), -0.2, 0.2)), 2.9999999242136255e-05, 5.999999848427251e-05),
        "second_q": set_ends(jax.random.randint(streams_of[6], (HOT, D, F), 32, 128), jax.random.fold_in(streams_of[6], 1), 32, 127).astype(jnp.int32),
        "second_scale": jnp.clip(jnp.exp(math.log(7.999999773744548e-09) - 0.98082922 * jax.random.uniform(streams_of[7], (HOT, D, F // QBLOCK), jnp.float32) ** block_levels(streams_of[7], (HOT, D, F // QBLOCK), ((1, 8),), -0.2, 0.2)), 3.000000026176508e-09, 7.999999773744548e-09),
    }


BETA_ONE = 0.9
BETA_TWO = 0.95
CORR_ONE = 1.0 - 0.9 ** 10
CORR_TWO = 1.0 - 0.95 ** 10
EPSILON = 1e-08
RATE = 0.002

def dequant(quant, scale):
    shaped = quant.astype(jnp.float32).reshape(quant.shape[0], quant.shape[1], -1, QBLOCK)
    return (shaped * scale[..., None]).reshape(quant.shape)

def adam_update(weight, grad, first_q, first_scale, second_q, second_scale):
    first = BETA_ONE * dequant(first_q, first_scale) + (1.0 - BETA_ONE) * grad
    second = BETA_TWO * dequant(second_q, second_scale) + (1.0 - BETA_TWO) * grad * grad
    step = first / CORR_ONE / (jnp.sqrt(second / CORR_TWO) + EPSILON)
    return (step, weight - RATE * step)

def reference(tokens, route, cotangent, weight, first_q, first_scale, second_q, second_scale):
    devices = N_REP * N_EP
    pool = tokens.reshape(devices, TOK_DEV, D)
    routes = route.reshape(HOT, devices, ROWS).transpose(1, 0, 2)
    cots = cotangent.reshape(HOT, devices, ROWS, F).transpose(1, 0, 2, 3)
    weight_b = weight.astype(jnp.bfloat16).astype(jnp.float32)
    high = lax.Precision.HIGHEST

    def one_device(total, items):
        pool_dev, route_dev, cot_dev = items
        chosen = pool_dev[route_dev].astype(jnp.float32)
        gate = jnp.einsum('erd,edf->erf', chosen, weight_b, precision=high)
        sig = jax.nn.sigmoid(gate)
        dgate = (cot_dev.astype(jnp.float32) * sig * (1.0 + gate * (1.0 - sig))).astype(jnp.bfloat16).astype(jnp.float32)
        dx = jnp.einsum('erf,edf->erd', dgate, weight_b, precision=high)
        grads = jnp.zeros((TOK_DEV, D), jnp.float32).at[route_dev.reshape(-1)].add(dx.reshape(-1, D))
        total = total + jnp.einsum('erd,erf->edf', chosen, dgate, precision=high)
        return (total, grads.astype(jnp.bfloat16))
    summed, token_grad = lax.scan(one_device, jnp.zeros((HOT, D, F), jnp.float32), (pool, routes, cots))
    grad = summed / ALL_ROWS
    step_dir, new_weight = adam_update(weight, grad, first_q, first_scale, second_q, second_scale)
    new_b = new_weight.astype(jnp.bfloat16).astype(jnp.float32)

    def rerun(items):
        pool_dev, route_dev = items
        chosen = pool_dev[route_dev].astype(jnp.float32)
        return jnp.einsum('erd,edf->erf', chosen, new_b, precision=high).astype(jnp.bfloat16)
    nexts = lax.map(rerun, (pool, routes))
    next_gate = nexts.transpose(1, 0, 2, 3).reshape(HOT, ALL_ROWS, F)
    return (token_grad.reshape(TOKENS, D), step_dir, new_weight, next_gate)
```

```python
import jax
import jax.numpy as jnp
from jax import lax
from jax.sharding import PartitionSpec as P

QBLOCK = 128
BETA_ONE = 0.9
BETA_TWO = 0.95
CORR_ONE = 1.0 - 0.9**10
CORR_TWO = 1.0 - 0.95**10
EPSILON = 1e-08
RATE = 0.002
BF = jnp.bfloat16
F32 = jnp.float32


def dequant(quant, scale):
    shaped = quant.astype(F32).reshape(quant.shape[0], quant.shape[1], -1, QBLOCK)
    return (shaped * scale[..., None]).reshape(quant.shape)


def adam_update(weight, grad, first_q, first_scale, second_q, second_scale):
    first = BETA_ONE * dequant(first_q, first_scale) + (1.0 - BETA_ONE) * grad
    second = BETA_TWO * dequant(second_q, second_scale) + (1.0 - BETA_TWO) * grad * grad
    step = first / CORR_ONE / (jnp.sqrt(second / CORR_TWO) + EPSILON)
    return (step, weight - RATE * step)


def on_device(tokens, route, cotangent, weight, first_q, first_scale, second_q, second_scale):
    n_rep = lax.axis_size("rep")
    n_ep = lax.axis_size("ep")
    experts, rows_here = route.shape
    count, width = tokens.shape
    feature = cotangent.shape[2]
    owned = weight.shape[1]
    piece = owned // n_rep
    total_rows = rows_here * n_rep * n_ep
    whole = lax.all_gather(weight.astype(BF), "ep", axis=1, tiled=True)
    spots = lax.broadcasted_iota(jnp.int32, (experts, count, rows_here), 1)
    pick = (spots == route[:, None, :]).astype(BF)
    cot = jnp.einsum("etr,erf->etf", pick, cotangent, preferred_element_type=F32)
    gate = jnp.einsum("td,edf->etf", tokens, whole, preferred_element_type=F32)
    sig = jax.nn.sigmoid(gate)
    dgate = (cot * sig * (1.0 + gate * (1.0 - sig))).astype(BF)
    partial = jnp.einsum("td,etf->edf", tokens, dgate, preferred_element_type=F32).astype(BF)
    shuffled = (
        partial.reshape(experts, n_ep, n_rep, piece, feature)
        .transpose(2, 1, 3, 0, 4)
        .reshape(n_rep * n_ep * piece, experts * feature)
    )
    quarter = lax.psum_scatter(shuffled, "rep", scatter_dimension=0, tiled=True)
    summed = lax.psum_scatter(quarter, "ep", scatter_dimension=0, tiled=True)
    token_grad = jnp.einsum("etf,edf->td", dgate, whole, preferred_element_type=F32).astype(BF)
    grad = lax.all_gather(summed, "rep", axis=0, tiled=True).astype(F32)
    grad = grad.reshape(owned, experts, feature).transpose(1, 0, 2) / total_rows
    step_dir, new_weight = adam_update(
        weight, grad, first_q, first_scale, second_q, second_scale
    )
    new_whole = lax.all_gather(new_weight.astype(BF), "ep", axis=1, tiled=True)
    nexts = jnp.einsum("td,edf->etf", tokens, new_whole, preferred_element_type=F32).astype(BF)
    next_gate = jnp.einsum("etr,etf->erf", pick, nexts, preferred_element_type=F32).astype(BF)
    return (token_grad, step_dir, new_weight, next_gate)


def solution(mesh):
    in_specs = (
        P(("rep", "ep"), None),
        P(None, ("rep", "ep")),
        P(None, ("rep", "ep"), None),
        P(None, "ep", None),
        P(None, "ep", None),
        P(None, "ep", None),
        P(None, "ep", None),
        P(None, "ep", None),
    )
    out_specs = (
        P(("rep", "ep"), None),
        P(None, "ep", None),
        P(None, "ep", None),
        P(None, ("rep", "ep"), None),
    )
    return jax.shard_map(
        on_device, mesh=mesh, in_specs=in_specs, out_specs=out_specs, check_vma=False
    )
```

```python
import functools

import jax
import jax.numpy as jnp
from jax import lax
from jax.experimental import pallas as pl
from jax.experimental.pallas import tpu as pltpu
from jax.sharding import PartitionSpec as P

QBLOCK = 128
BETA_ONE = 0.9
BETA_TWO = 0.95
CORR_ONE = 1.0 - 0.9**10
CORR_TWO = 1.0 - 0.95**10
EPSILON = 1e-08
RATE = 0.002
BF = jnp.bfloat16
F32 = jnp.float32

MESH = pl.DeviceIdType.MESH
TILE = 16


class Spot:
    def __init__(self, n_ep, height):
        self.rep, self.ep = lax.axis_index("rep"), lax.axis_index("ep")
        self.core, self.y = self.rep % 2, self.rep // 2
        self.x, self.z = self.ep % 2, self.ep // 2
        self.n_ep, self.line, self.height = n_ep, n_ep // 2, height
        self.alone = height // TILE * 3 // 8 * TILE
        self.held = height - self.alone
        self.both = self.held - self.alone
        self.start = self.y * self.alone
        self.x_peer = (self.rep, self.z * 2 + 1 - self.x)
        self.y_peer = ((1 - self.y) * 2 + self.core, self.ep)
        self.core_peer = (self.y * 2 + 1 - self.core, self.ep)
        self.order = []
        for k in range(1, self.line // 2 + 1):
            self.order += [k] if k == self.line - k else [k, self.line - k]

    def z_peer(self, k):
        return (self.rep, (self.z + k) % self.line * 2 + self.x)

    def meet(self):
        barrier = pltpu.get_barrier_semaphore()
        peers = [self.z_peer(k) for k in range(1, self.line)]
        peers += [self.x_peer, self.y_peer, self.core_peer]
        for peer in peers:
            pl.semaphore_signal(barrier, inc=1, device_id=peer, device_id_type=MESH)
        pl.semaphore_wait(barrier, len(peers))


def tiled(value):
    return pl.multiple_of(value, TILE)


def remote(src, dst, send, recv, peer):
    return pltpu.make_async_remote_copy(
        src_ref=src, dst_ref=dst, send_sem=send, recv_sem=recv, device_id=peer, device_id_type=MESH
    )


class Gather:
    def __init__(self, at, own, out, sems):
        self.at, self.own, self.out = at, own, out
        (self.zs, self.xs, self.ys, self.c1s, self.c2s, self.r1, self.r2, self.r3, self.r4) = sems
        self.sent = []

    def part(self, half, ep, first, rows):
        return self.out.at[half, pl.ds(tiled(ep * self.at.height + first), rows)]

    def mine(self, ep):
        return self.part(self.at.core, ep, self.at.start, self.at.held)

    def go(self, src, dst, send, recv, peer):
        copy = remote(src, dst, send, recv, peer)
        copy.start()
        self.sent.append(copy)

    def start(self):
        at = self.at
        at.meet()
        src = self.own.at[at.core, pl.ds(tiled(at.start), at.held)]
        for k in at.order:
            self.go(src, self.mine(at.ep), self.zs.at[k], self.r1.at[at.ep], at.z_peer(k))
        self.go(src, self.mine(at.ep), self.xs.at[0], self.r1.at[at.ep], at.x_peer)

    def arrive(self, dst, recv):
        at = self.at
        remote(dst, dst, self.zs.at[0], recv, at.x_peer).wait_recv()

    def share(self, ep):
        at = self.at
        if at.alone:
            rows = self.part(at.core, ep, at.y * at.held, at.alone)
            self.go(rows, rows, self.ys.at[ep], self.r2.at[ep], at.y_peer)
        self.go(self.mine(ep), self.mine(ep), self.c1s.at[ep], self.r3.at[ep], at.core_peer)

    def from_line(self, k):
        at = self.at
        ep = (at.z + at.line - k) % at.line * 2 + at.x
        self.arrive(self.mine(ep), self.r1.at[ep])
        self.go(self.mine(ep), self.mine(ep), self.xs.at[k], self.r1.at[ep], at.x_peer)
        self.share(ep)

    def from_pair(self, k):
        at = self.at
        ep = (at.z + at.line - k) % at.line * 2 + 1 - at.x
        self.arrive(self.mine(ep), self.r1.at[ep])
        self.share(ep)

    def relay(self):
        at = self.at
        waiting = [0] + at.order
        for k in at.order:
            self.from_line(k)
            self.from_pair(waiting.pop(0))
        for k in waiting:
            self.from_pair(k)
        if at.alone:
            for ep in self.others():
                rows = self.part(at.core, ep, (1 - at.y) * at.held, at.alone)
                self.arrive(rows, self.r2.at[ep])
                self.go(rows, rows, self.c2s.at[ep], self.r4.at[ep], at.core_peer)

    def others(self):
        at = self.at
        found = []
        waiting = [0] + at.order
        for k in at.order:
            found.append((at.z + at.line - k) % at.line * 2 + at.x)
            found.append((at.z + at.line - waiting.pop(0)) % at.line * 2 + 1 - at.x)
        for k in waiting:
            found.append((at.z + at.line - k) % at.line * 2 + 1 - at.x)
        return found

    def whole(self, ep):
        at = self.at
        self.arrive(self.part(1 - at.core, ep, at.start, at.held), self.r3.at[ep])
        if at.alone:
            self.arrive(
                self.part(1 - at.core, ep, (1 - at.y) * at.held, at.alone), self.r4.at[ep]
            )

    def end(self):
        for copy in self.sent:
            copy.wait_send()


def gather_sems(n_ep):
    line = n_ep // 2
    return [pltpu.SemaphoreType.DMA((line,)), pltpu.SemaphoreType.DMA((line,))] + [
        pltpu.SemaphoreType.DMA((n_ep,)) for _ in range(7)
    ]


def gather_kernel(n_ep, own, out, *sems):
    at = Spot(n_ep, own.shape[1])
    job = Gather(at, own, out, sems)
    job.start()
    out[:, pl.ds(tiled(at.ep * at.height), at.height)] = own[...]
    job.relay()
    for ep in job.others():
        job.whole(ep)
    job.end()


def gather_blocks(own, n_ep, tag):
    halves, height, feature = own.shape
    return pl.pallas_call(
        functools.partial(gather_kernel, n_ep),
        out_shape=jax.ShapeDtypeStruct((halves, n_ep * height, feature), own.dtype),
        in_specs=[pl.BlockSpec(memory_space=pltpu.VMEM)],
        out_specs=pl.BlockSpec(memory_space=pltpu.VMEM),
        scratch_shapes=gather_sems(n_ep),
        compiler_params=pltpu.CompilerParams(collective_id=tag, has_side_effects=True),
        name=f"gather_{tag}",
    )(own)


class Reduce:
    def __init__(self, at, inp, out, bufs, sems):
        self.at, self.inp, self.out = at, inp, out
        (self.bc, self.s1, self.by, self.s2, self.bx, self.bz, self.fin, self.by2) = bufs
        (self.cs, self.cr, self.ys, self.yr, self.xs, self.xr, self.zs, self.zr, self.fs, self.fr) = sems

    def block(self, i):
        at = self.at
        far = jnp.where(i < at.line, 1, 0)
        z = (at.z + 1 + i) % at.line
        x = at.x + far - 2 * at.x * far
        return z, z * 2 + x

    def core_copy(self, ep):
        at = self.at
        return remote(
            self.inp.at[1 - at.core, pl.ds(tiled(ep * at.height), at.height)],
            self.bc.at[ep],
            self.cs.at[ep],
            self.cr.at[ep],
            at.core_peer,
        )

    def y_copy(self, ep):
        at = self.at
        return remote(
            self.s1.at[ep, pl.ds(tiled((1 - at.y) * at.held), at.alone)],
            self.by.at[ep],
            self.ys.at[ep],
            self.yr.at[ep],
            at.y_peer,
        )

    def x_copy(self, z, ep):
        return remote(self.s2.at[ep], self.bx.at[z], self.xs.at[z], self.xr.at[z], self.at.x_peer)

    def z_copy(self, k, ep):
        at = self.at
        return remote(self.s2.at[ep], self.bz.at[k], self.zs.at[k], self.zr.at[k], at.z_peer(k))

    def first(self, i):
        at = self.at
        _, ep = self.block(i)
        self.core_copy(ep).wait_recv()
        here = self.inp[at.core, pl.ds(tiled(ep * at.height), at.height)].astype(F32)
        self.s1[ep] = (here + self.bc[ep].astype(F32)).astype(BF)
        if at.alone:
            self.y_copy(ep).start()

    def pieces(self, ep):
        at = self.at
        found = []
        if at.alone:
            self.y_copy(ep).wait_recv()
            value = self.s1[ep, pl.ds(tiled(at.y * at.held), at.alone)].astype(F32)
            found.append((tiled(at.y * at.both), at.alone, value + self.by[ep].astype(F32)))
        value = self.s1[ep, pl.ds(at.alone, at.both)].astype(F32)
        found.append((tiled((1 - at.y) * at.alone), at.both, value))
        return found

    def second_far(self, i):
        z, ep = self.block(i)
        for first, rows, value in self.pieces(ep):
            self.s2[ep, pl.ds(first, rows)] = value.astype(BF)
        self.x_copy(z, ep).start()

    def second_near(self, i):
        z, ep = self.block(i)
        found = self.pieces(ep)
        self.x_copy(z, ep).wait_recv()
        for first, rows, value in found:
            total = value + self.bx[z, pl.ds(first, rows)].astype(F32)
            self.s2[ep, pl.ds(first, rows)] = total.astype(BF)

    def start(self):
        at = self.at
        at.meet()

        @pl.loop(0, at.n_ep)
        def _(i):
            _, ep = self.block(i)
            self.core_copy(ep).start()

    def run(self, lag=3):
        at = self.at
        for i in range(min(lag, at.n_ep)):
            self.first(i)

        @pl.loop(0, at.line)
        def _(i):
            @pl.when(i + lag < at.n_ep)
            def _():
                self.first(i + lag)

            self.second_far(i)

        @pl.loop(at.line, at.n_ep - 1)
        def _(i):
            @pl.when(i + lag < at.n_ep)
            def _():
                self.first(i + lag)

            self.second_near(i)
            k = i - at.line + 1
            _, ep = self.block(i)
            self.z_copy(k, ep).start()

        self.second_near(at.n_ep - 1)

    def finish(self):
        at = self.at
        total = self.s2[at.ep].astype(F32)
        for k in range(1, at.line):
            self.z_copy(k, at.ep).wait_recv()
            total += self.bz[k].astype(F32)
        self.fin[...] = total.astype(BF)
        swap = remote(self.fin, self.by2, self.fs.at[0], self.fr.at[0], at.y_peer)
        swap.start()
        half = self.out.at[at.core]
        if at.alone:
            half[pl.ds(tiled(at.y * at.held), at.alone)] = self.fin[
                pl.ds(tiled(at.y * at.both), at.alone)
            ]
        swap.wait()
        if at.alone:
            half[pl.ds(tiled((1 - at.y) * at.held), at.alone)] = self.by2[
                pl.ds(tiled((1 - at.y) * at.both), at.alone)
            ]
        here = self.fin[pl.ds(tiled((1 - at.y) * at.alone), at.both)].astype(F32)
        there = self.by2[pl.ds(tiled(at.y * at.alone), at.both)].astype(F32)
        half[pl.ds(at.alone, at.both)] = (here + there).astype(BF)
        last = remote(half, half, self.fs.at[1], self.fr.at[1], at.core_peer)
        last.start()
        last.wait_send()
        other = self.out.at[1 - at.core]
        remote(other, other, self.fs.at[1], self.fr.at[1], at.core_peer).wait_recv()

        @pl.loop(0, at.n_ep)
        def _(i):
            _, ep = self.block(i)
            self.core_copy(ep).wait_send()
            if at.alone:
                self.y_copy(ep).wait_send()

        @pl.loop(0, at.line)
        def _(i):
            z, ep = self.block(i)
            self.x_copy(z, ep).wait_send()

        @pl.loop(1, at.line)
        def _(k):
            self.z_copy(k, at.ep).wait_send()


def reduce_bufs(n_ep, height, feature):
    line = n_ep // 2
    alone = height // TILE * 3 // 8 * TILE
    held = height - alone
    shapes = [
        (n_ep, height),
        (n_ep, height),
        (n_ep, max(alone, TILE)),
        (n_ep, held),
        (line, held),
        (line, held),
        (held,),
        (held,),
    ]
    counts = [n_ep, n_ep, n_ep, n_ep, line, line, line, line, 2, 2]
    return [pltpu.VMEM(s + (feature,), BF) for s in shapes] + [
        pltpu.SemaphoreType.DMA((c,)) for c in counts
    ]


def reduce_kernel(n_ep, inp, out, *scratch):
    at = Spot(n_ep, out.shape[1])
    job = Reduce(at, inp, out, scratch[:8], scratch[8:])
    job.start()
    job.run()
    job.finish()


def reduce_blocks(inp, n_ep, tag):
    halves, width, feature = inp.shape
    height = width // n_ep
    return pl.pallas_call(
        functools.partial(reduce_kernel, n_ep),
        out_shape=jax.ShapeDtypeStruct((halves, height, feature), inp.dtype),
        in_specs=[pl.BlockSpec(memory_space=pltpu.VMEM)],
        out_specs=pl.BlockSpec(memory_space=pltpu.VMEM),
        scratch_shapes=reduce_bufs(n_ep, height, feature),
        compiler_params=pltpu.CompilerParams(collective_id=tag, has_side_effects=True),
        name=f"reduce_{tag}",
    )(inp)


def dequant(quant, scale):
    shaped = quant.astype(F32).reshape(quant.shape[0], quant.shape[1], -1, QBLOCK)
    return (shaped * scale[..., None]).reshape(quant.shape)


def adam_update(weight, grad, first_q, first_scale, second_q, second_scale):
    first = BETA_ONE * dequant(first_q, first_scale) + (1.0 - BETA_ONE) * grad
    second = BETA_TWO * dequant(second_q, second_scale) + (1.0 - BETA_TWO) * grad * grad
    step = first / CORR_ONE / (jnp.sqrt(second / CORR_TWO) + EPSILON)
    return (step, weight - RATE * step)


def on_device(tokens, route, cotangent, weight, first_q, first_scale, second_q, second_scale):
    n_rep = lax.axis_size("rep")
    n_ep = lax.axis_size("ep")
    experts, rows_here = route.shape
    count, width = tokens.shape
    feature = cotangent.shape[2]
    total_rows = rows_here * n_rep * n_ep
    whole = gather_blocks(weight.astype(BF), n_ep, 1)
    spots = lax.broadcasted_iota(jnp.int32, (experts, count, rows_here), 1)
    pick = (spots == route[:, None, :]).astype(BF)
    cot = jnp.einsum("etr,erf->etf", pick, cotangent, preferred_element_type=F32)
    gate = jnp.einsum("td,edf->etf", tokens, whole, preferred_element_type=F32)
    sig = jax.nn.sigmoid(gate)
    dgate = (cot * sig * (1.0 + gate * (1.0 - sig))).astype(BF)
    partial = jnp.einsum("td,etf->edf", tokens, dgate, preferred_element_type=F32).astype(BF)
    grad = reduce_blocks(partial, n_ep, 2).astype(F32) / total_rows
    token_grad = jnp.einsum("etf,edf->td", dgate, whole, preferred_element_type=F32).astype(BF)
    step_dir, new_weight = adam_update(
        weight, grad, first_q, first_scale, second_q, second_scale
    )
    new_whole = gather_blocks(new_weight.astype(BF), n_ep, 3)
    nexts = jnp.einsum("td,edf->etf", tokens, new_whole, preferred_element_type=F32).astype(BF)
    next_gate = jnp.einsum("etr,etf->erf", pick, nexts, preferred_element_type=F32).astype(BF)
    return (token_grad, step_dir, new_weight, next_gate)


def solution(mesh):
    in_specs = (
        P(("rep", "ep"), None),
        P(None, ("rep", "ep")),
        P(None, ("rep", "ep"), None),
        P(None, "ep", None),
        P(None, "ep", None),
        P(None, "ep", None),
        P(None, "ep", None),
        P(None, "ep", None),
    )
    out_specs = (
        P(("rep", "ep"), None),
        P(None, "ep", None),
        P(None, "ep", None),
        P(None, ("rep", "ep"), None),
    )
    return jax.shard_map(
        on_device, mesh=mesh, in_specs=in_specs, out_specs=out_specs, check_vma=False
    )
```

```python
import functools

import jax
import jax.numpy as jnp
from jax import lax
from jax.experimental import pallas as pl
from jax.experimental.pallas import tpu as pltpu
from jax.sharding import PartitionSpec as P

QBLOCK = 128
BETA_ONE = 0.9
BETA_TWO = 0.95
CORR_ONE = 1.0 - 0.9**10
CORR_TWO = 1.0 - 0.95**10
EPSILON = 1e-08
RATE = 0.002
BF = jnp.bfloat16
F32 = jnp.float32

MESH = pl.DeviceIdType.MESH
TILE = 16


class Spot:
    def __init__(self, n_ep, height):
        self.rep, self.ep = lax.axis_index("rep"), lax.axis_index("ep")
        self.core, self.y = self.rep % 2, self.rep // 2
        self.x, self.z = self.ep % 2, self.ep // 2
        self.n_ep, self.line, self.height = n_ep, n_ep // 2, height
        self.alone = height // TILE * 3 // 8 * TILE
        self.held = height - self.alone
        self.both = self.held - self.alone
        self.start = self.y * self.alone
        self.x_peer = (self.rep, self.z * 2 + 1 - self.x)
        self.y_peer = ((1 - self.y) * 2 + self.core, self.ep)
        self.core_peer = (self.y * 2 + 1 - self.core, self.ep)
        self.order = []
        for k in range(1, self.line // 2 + 1):
            self.order += [k] if k == self.line - k else [k, self.line - k]

    def near(self, j):
        last = self.line - 1
        few = jnp.where(2 * self.z < last, self.z, last - self.z)
        far = jnp.where(2 * self.z < last, 1, -1)
        sign = jnp.where(j < 2 * few, 1 - 2 * (j % 2), far)
        return self.z + sign * jnp.where(j < 2 * few, j // 2 + 1, j - few + 1), sign

    def z_peer(self, k):
        return (self.rep, (self.z + k) % self.line * 2 + self.x)

    def meet(self):
        barrier = pltpu.get_barrier_semaphore()
        peers = [self.z_peer(k) for k in range(1, self.line)]
        peers += [self.x_peer, self.y_peer, self.core_peer]
        for peer in peers:
            pl.semaphore_signal(barrier, inc=1, device_id=peer, device_id_type=MESH)
        pl.semaphore_wait(barrier, len(peers))


def tiled(value):
    return pl.multiple_of(value, TILE)


def remote(src, dst, send, recv, peer):
    return pltpu.make_async_remote_copy(
        src_ref=src, dst_ref=dst, send_sem=send, recv_sem=recv, device_id=peer, device_id_type=MESH
    )


class Gather:
    def __init__(self, at, own, out, sems):
        self.at, self.own, self.out = at, own, out
        (self.zs, self.xs, self.ys, self.c1s, self.c2s, self.r1, self.r2, self.r3, self.r4) = sems

    def part(self, half, ep, first, rows):
        return self.out.at[half, pl.ds(tiled(ep * self.at.height + first), rows)]

    def mine(self, ep):
        return self.part(self.at.core, ep, self.at.start, self.at.held)

    def first_copies(self, act):
        at = self.at
        src = self.own.at[at.core, pl.ds(tiled(at.start), at.held)]

        def to(sem, peer):
            return remote(src, self.mine(at.ep), sem, self.r1.at[at.ep], peer)

        @pl.when(at.z + 1 < at.line)
        def _():
            act(to(self.zs.at[at.line - 1], at.z_peer(1)))

        @pl.when(at.z > 0)
        def _():
            act(to(self.zs.at[at.line], at.z_peer(at.line - 1)))

        act(to(self.xs.at[at.line - 1], at.x_peer))

    def line_copies(self, j, act):
        at = self.at
        z, sign = at.near(j)
        ep = z * 2 + at.x
        rows = self.mine(ep)
        onward = at.z - sign

        @pl.when((onward >= 0) & (onward < at.line))
        def _():
            peer = (at.rep, onward * 2 + at.x)
            act(remote(rows, rows, self.zs.at[j], self.r1.at[ep], peer))

        act(remote(rows, rows, self.xs.at[j], self.r1.at[ep], at.x_peer))

    def share_copies(self, ep, act):
        at = self.at
        if at.alone:
            rows = self.part(at.core, ep, at.y * at.held, at.alone)
            act(remote(rows, rows, self.ys.at[ep], self.r2.at[ep], at.y_peer))
        act(remote(self.mine(ep), self.mine(ep), self.c1s.at[ep], self.r3.at[ep], at.core_peer))

    def late_copy(self, ep):
        at = self.at
        rows = self.part(at.core, ep, (1 - at.y) * at.held, at.alone)
        return remote(rows, rows, self.c2s.at[ep], self.r4.at[ep], at.core_peer)

    def arrive(self, dst, recv):
        remote(dst, dst, self.zs.at[0], recv, self.at.x_peer).wait_recv()

    def start(self):
        self.first_copies(lambda copy: copy.start())

    def from_line(self, j):
        at = self.at
        ep = at.near(j)[0] * 2 + at.x
        self.arrive(self.mine(ep), self.r1.at[ep])
        self.line_copies(j, lambda copy: copy.start())
        self.share_copies(ep, lambda copy: copy.start())
        return ep

    def from_pair(self, j):
        at = self.at
        ep = (at.z if j < 0 else at.near(j)[0]) * 2 + 1 - at.x
        self.arrive(self.mine(ep), self.r1.at[ep])
        self.share_copies(ep, lambda copy: copy.start())
        return ep

    def late(self, ep):
        at = self.at
        if at.alone:
            rows = self.part(at.core, ep, (1 - at.y) * at.held, at.alone)
            self.arrive(rows, self.r2.at[ep])
            self.late_copy(ep).start()

    def whole(self, ep):
        at = self.at
        self.arrive(self.part(1 - at.core, ep, at.start, at.held), self.r3.at[ep])
        if at.alone:
            rows = self.part(1 - at.core, ep, (1 - at.y) * at.held, at.alone)
            self.arrive(rows, self.r4.at[ep])

    def relay(self, tasks, use):
        at = self.at
        tasks = list(tasks)
        order = []
        for j in range(at.line - 1):
            for step, k in ((self.from_line, j), (self.from_pair, j - 1)):
                order.append(step(k))
                if tasks:
                    tasks.pop(0)()
        order.append(self.from_pair(at.line - 2))
        for task in tasks:
            task()
        behind = None
        for ep in order:
            self.late(ep)
            if behind is not None:
                self.whole(behind)
                use(behind)
            behind = ep
        self.whole(behind)
        use(behind)

    def end(self):
        at = self.at

        def done(copy):
            copy.wait_send()

        self.first_copies(done)
        for j in range(at.line - 1):
            self.line_copies(j, done)

        @pl.loop(1, at.n_ep)
        def _(k):
            ep = (at.ep + k) % at.n_ep
            self.share_copies(ep, done)
            if at.alone:
                self.late_copy(ep).wait_send()


def gather_sems(n_ep):
    line = n_ep // 2
    return [pltpu.SemaphoreType.DMA((line + 1,)), pltpu.SemaphoreType.DMA((line,))] + [
        pltpu.SemaphoreType.DMA((n_ep,)) for _ in range(7)
    ]


class Reduce:
    def __init__(self, at, term, fill, inp, out, bufs, sems):
        self.at, self.term, self.fill, self.inp, self.out = at, term, fill, inp, out
        (self.bc, self.s1, self.by, self.s2, self.bx, self.bz, self.fin, self.by2) = bufs
        (self.cs, self.cr, self.ys, self.yr, self.xs, self.xr, self.zs, self.zr, self.fs, self.fr) = sems

    def block(self, i):
        at = self.at
        far = jnp.where(i < at.line, 1, 0)
        z = (at.z + 1 + i) % at.line
        x = at.x + far - 2 * at.x * far
        return z, z * 2 + x

    def core_copy(self, ep):
        at = self.at
        return remote(
            self.inp.at[1 - at.core, pl.ds(tiled(ep * at.height), at.height)],
            self.bc.at[ep],
            self.cs.at[ep],
            self.cr.at[ep],
            at.core_peer,
        )

    def y_copy(self, ep):
        at = self.at
        return remote(
            self.s1.at[ep, pl.ds(tiled((1 - at.y) * at.held), at.alone)],
            self.by.at[ep],
            self.ys.at[ep],
            self.yr.at[ep],
            at.y_peer,
        )

    def x_copy(self, z, ep):
        return remote(self.s2.at[ep], self.bx.at[z], self.xs.at[z], self.xr.at[z], self.at.x_peer)

    def z_copy(self, k, ep):
        at = self.at
        return remote(self.s2.at[ep], self.bz.at[k], self.zs.at[k], self.zr.at[k], at.z_peer(k))

    def first(self, i):
        at = self.at
        _, ep = self.block(i)
        self.core_copy(ep).wait_recv()
        here = self.inp[at.core, pl.ds(tiled(ep * at.height), at.height)].astype(F32)
        self.s1[ep] = (here + self.bc[ep].astype(F32)).astype(BF)
        if at.alone:
            self.y_copy(ep).start()

    def pieces(self, ep):
        at = self.at
        found = []
        if at.alone:
            self.y_copy(ep).wait_recv()
            value = self.s1[ep, pl.ds(tiled(at.y * at.held), at.alone)].astype(F32)
            found.append((tiled(at.y * at.both), at.alone, value + self.by[ep].astype(F32)))
        value = self.s1[ep, pl.ds(at.alone, at.both)].astype(F32)
        found.append((tiled((1 - at.y) * at.alone), at.both, value))
        return found

    def second_far(self, i):
        z, ep = self.block(i)
        for first, rows, value in self.pieces(ep):
            self.s2[ep, pl.ds(first, rows)] = value.astype(BF)
        self.x_copy(z, ep).start()

    def second_near(self, i):
        z, ep = self.block(i)
        found = self.pieces(ep)
        self.x_copy(z, ep).wait_recv()
        for first, rows, value in found:
            total = value + self.bx[z, pl.ds(first, rows)].astype(F32)
            self.s2[ep, pl.ds(first, rows)] = total.astype(BF)

    def make(self, i):
        at = self.at
        _, ep = self.block(i)
        rows = pl.ds(tiled(ep * at.height), at.height)
        self.inp[1 - at.core, rows] = self.term(1 - at.core, rows).astype(BF)
        self.core_copy(ep).start()
        self.inp[at.core, rows] = self.term(at.core, rows).astype(BF)

    def ahead(self, i, lag):
        @pl.when(i + 2 * lag < self.at.n_ep)
        def _():
            self.make(i + 2 * lag)

        @pl.when(i + lag < self.at.n_ep)
        def _():
            self.first(i + lag)

    def run(self, lag=2):
        at = self.at
        self.make(0)
        for i in range(lag):
            for j in range(2 * i + 1, min(2 * i + 3, 2 * lag)):
                self.make(j)
            self.first(i)

        @pl.loop(0, at.line)
        def _(i):
            self.ahead(i, lag)
            self.second_far(i)
            self.fill(i)

        @pl.loop(at.line, at.n_ep - 1)
        def _(i):
            self.ahead(i, lag)
            self.second_near(i)
            k = i - at.line + 1
            _, ep = self.block(i)
            self.z_copy(k, ep).start()
            self.fill(i)

        self.second_near(at.n_ep - 1)
        self.fill(at.n_ep - 1)

    def finish(self):
        at = self.at
        total = self.s2[at.ep].astype(F32)
        for k in range(1, at.line):
            self.z_copy(k, at.ep).wait_recv()
            total += self.bz[k].astype(F32)
        self.fin[...] = total.astype(BF)
        swap = remote(self.fin, self.by2, self.fs.at[0], self.fr.at[0], at.y_peer)
        swap.start()
        half = self.out.at[at.core]
        if at.alone:
            half[pl.ds(tiled(at.y * at.held), at.alone)] = self.fin[
                pl.ds(tiled(at.y * at.both), at.alone)
            ]
        swap.wait()
        if at.alone:
            half[pl.ds(tiled((1 - at.y) * at.held), at.alone)] = self.by2[
                pl.ds(tiled((1 - at.y) * at.both), at.alone)
            ]
        here = self.fin[pl.ds(tiled((1 - at.y) * at.alone), at.both)].astype(F32)
        there = self.by2[pl.ds(tiled(at.y * at.alone), at.both)].astype(F32)
        half[pl.ds(at.alone, at.both)] = (here + there).astype(BF)
        last = remote(half, half, self.fs.at[1], self.fr.at[1], at.core_peer)
        last.start()
        last.wait_send()
        other = self.out.at[1 - at.core]
        remote(other, other, self.fs.at[1], self.fr.at[1], at.core_peer).wait_recv()

        @pl.loop(0, at.n_ep)
        def _(i):
            _, ep = self.block(i)
            self.core_copy(ep).wait_send()
            if at.alone:
                self.y_copy(ep).wait_send()

        @pl.loop(0, at.line)
        def _(i):
            z, ep = self.block(i)
            self.x_copy(z, ep).wait_send()

        @pl.loop(1, at.line)
        def _(k):
            self.z_copy(k, at.ep).wait_send()


def reduce_bufs(n_ep, height, feature):
    line = n_ep // 2
    alone = height // TILE * 3 // 8 * TILE
    held = height - alone
    shapes = [
        (n_ep, height),
        (n_ep, height),
        (n_ep, max(alone, TILE)),
        (n_ep, held),
        (line, held),
        (line, held),
        (held,),
        (held,),
    ]
    counts = [n_ep, n_ep, n_ep, n_ep, line, line, line, line, 2, 2]
    return [pltpu.VMEM(s + (feature,), BF) for s in shapes] + [
        pltpu.SemaphoreType.DMA((c,)) for c in counts
    ]


CHUNK = 256
LANES = 128


def dot(a, b, dims=((1,), (0,))):
    return lax.dot_general(a, b, (dims, ((), ())), preferred_element_type=F32)


def step_kernel(n_ep, total_rows, *refs):
    (tokens, route, cot, own, weight, fq, fs, sq, ss) = refs[:9]
    (token_grad, step_dir, new_weight, next_gate) = refs[9:13]
    (pick, pick_t, tok_t, spread, acc, dgate, whole, again, inp, grad, own_b) = refs[13:24]
    bufs, sems = refs[24:32], refs[32:42]
    sems_one, sems_two = refs[42:51], refs[51:60]
    halves, height, feature = own.shape
    count, width = tokens.shape
    picked = route.shape[1]
    at = Spot(n_ep, height)
    by_block = height % LANES == 0

    def tiles(extent, body):
        size = CHUNK if extent % CHUNK == 0 else extent

        @pl.loop(0, extent // size)
        def _(t):
            body(pl.ds(pl.multiple_of(t * size, size), size))

    def project(half, cols, matrix, brows, fresh):
        def body(rows):
            value = dot(tokens[rows, cols], matrix[half, brows])
            acc[half, rows] = value if fresh else acc[half, rows] + value

        tiles(count, body)

    def use_block(matrix, ep, fresh=False):
        if by_block:
            spot = pl.ds(pl.multiple_of(ep * height, height), height)
            for half in range(halves):
                project(half, spot, matrix, spot, fresh)

    def use_rest(matrix):
        if not by_block:
            for half in range(halves):
                for j in range(width // CHUNK):
                    spot = pl.ds(j * CHUNK, CHUNK)
                    project(half, spot, matrix, spot, j == 0)

    def scatter(half):
        def body(rows):
            spots = lax.broadcasted_iota(jnp.int32, (rows.size, picked), 0) + rows.start
            hits = (spots == route[pl.ds(half, 1), :]).astype(F32).astype(BF)
            pick[half, rows] = hits
            spread[half, rows] = dot(hits, cot[half]).astype(BF)

        tiles(count, body)

    def flip_pick(half):
        pick_t[half] = pick[half].T

    def flip(j):
        spot = pl.ds(j * CHUNK, CHUNK)
        tok_t[spot, :] = tokens[:, spot].T

    def both(task, *args):
        for half in range(halves):
            task(half)

    own_rows = pl.ds(tiled(at.ep * height), height)
    one = Gather(at, own, whole, sems_one)
    at.meet()
    one.start()
    whole[:, own_rows] = own[...]
    flips = [functools.partial(flip, j) for j in range(width // CHUNK)]
    tasks = [functools.partial(scatter, h) for h in range(halves)]
    tasks.insert(1, lambda: use_block(whole, at.ep, True))
    tasks += [functools.partial(flip_pick, h) for h in range(halves)]
    while flips:
        pair = flips[:4]
        flips = flips[4:]
        tasks.append(lambda pair=pair: [f() for f in pair])
    one.relay(tasks, lambda ep: use_block(whole, ep))
    use_rest(whole)

    for half in range(halves):

        def shape_grad(rows):
            gate = acc[half, rows]
            sig = 1.0 / (1.0 + jnp.exp(-gate))
            value = spread[half, rows].astype(F32) * sig * (1.0 + gate * (1.0 - sig))
            dgate[half, rows] = value.astype(BF)

        tiles(count, shape_grad)

    def term(half, rows):
        return dot(tok_t[rows, :], dgate[half])

    def back(j):
        @pl.when(j < width // CHUNK)
        def _():
            spot = pl.ds(pl.multiple_of(j * CHUNK, CHUNK), CHUNK)

            def body(rows):
                value = dot(dgate[0, rows], whole[0, spot], ((1,), (1,)))
                for half in range(1, halves):
                    value += dot(dgate[half, rows], whole[half, spot], ((1,), (1,)))
                token_grad[rows, spot] = value.astype(BF)

            tiles(count, body)

    job = Reduce(at, term, back, inp, grad, bufs, sems)
    job.run()
    for j in range(n_ep, width // CHUNK):
        back(j)
    job.finish()

    slab = 64 if height % 64 == 0 else height
    for half in range(halves):

        @pl.loop(0, height // slab)
        def _(t):
            rows = pl.ds(pl.multiple_of(t * slab, slab), slab)
            for q in range(feature // QBLOCK):
                cols = pl.ds(q * QBLOCK, QBLOCK)
                here = (half, rows, cols)
                g = grad[here].astype(F32) / total_rows
                first = BETA_ONE * (fq[here].astype(F32) * fs[half, rows, pl.ds(q, 1)])
                second = BETA_TWO * (sq[here].astype(F32) * ss[half, rows, pl.ds(q, 1)])
                first += (1.0 - BETA_ONE) * g
                second += (1.0 - BETA_TWO) * g * g
                step = first / CORR_ONE / (jnp.sqrt(second / CORR_TWO) + EPSILON)
                fresh = weight[here] - RATE * step
                step_dir[here] = step
                new_weight[here] = fresh
                own_b[here] = fresh.astype(BF)

    two = Gather(at, own_b, again, sems_two)
    two.start()
    again[:, own_rows] = own_b[...]
    two.relay([lambda: use_block(again, at.ep, True)], lambda ep: use_block(again, ep))
    use_rest(again)
    for half in range(halves):
        rounded = acc[half].astype(BF)

        def put(rows):
            next_gate[half, rows] = dot(pick_t[half, rows], rounded).astype(BF)

        tiles(picked, put)
    one.end()
    two.end()


def on_device(tokens, route, cotangent, weight, first_q, first_scale, second_q, second_scale):
    n_rep = lax.axis_size("rep")
    n_ep = lax.axis_size("ep")
    halves, picked = route.shape
    count, width = tokens.shape
    feature = cotangent.shape[2]
    height = weight.shape[1]
    total_rows = picked * n_rep * n_ep
    vmem = pltpu.VMEM
    scratch = [
        vmem((halves, count, picked), BF),
        vmem((halves, picked, count), BF),
        vmem((width, count), BF),
        vmem((halves, count, feature), BF),
        vmem((halves, count, feature), F32),
        vmem((halves, count, feature), BF),
        vmem((halves, width, feature), BF),
        vmem((halves, width, feature), BF),
        vmem((halves, width, feature), BF),
        vmem((halves, height, feature), BF),
        vmem((halves, height, feature), BF),
    ]
    scratch += reduce_bufs(n_ep, height, feature) + gather_sems(n_ep) + gather_sems(n_ep)
    in_vmem = pl.BlockSpec(memory_space=pltpu.VMEM)
    return pl.pallas_call(
        functools.partial(step_kernel, n_ep, total_rows),
        out_shape=(
            jax.ShapeDtypeStruct(tokens.shape, BF),
            jax.ShapeDtypeStruct(weight.shape, F32),
            jax.ShapeDtypeStruct(weight.shape, F32),
            jax.ShapeDtypeStruct(cotangent.shape, BF),
        ),
        in_specs=[in_vmem] * 9,
        out_specs=(in_vmem,) * 4,
        scratch_shapes=scratch,
        compiler_params=pltpu.CompilerParams(
            collective_id=1, has_side_effects=True, vmem_limit_bytes=62 << 20
        ),
        name="hot_step",
    )(
        tokens, route, cotangent, weight.astype(BF),
        weight, first_q, first_scale, second_q, second_scale,
    )


def solution(mesh):
    in_specs = (
        P(("rep", "ep"), None),
        P(None, ("rep", "ep")),
        P(None, ("rep", "ep"), None),
        P(None, "ep", None),
        P(None, "ep", None),
        P(None, "ep", None),
        P(None, "ep", None),
        P(None, "ep", None),
    )
    out_specs = (
        P(("rep", "ep"), None),
        P(None, "ep", None),
        P(None, "ep", None),
        P(None, ("rep", "ep"), None),
    )
    return jax.shard_map(
        on_device, mesh=mesh, in_specs=in_specs, out_specs=out_specs, check_vma=False
    )
```

```python
import functools

import jax
import jax.numpy as jnp
from jax import lax
from jax.experimental import pallas as pl
from jax.experimental.pallas import tpu as pltpu
from jax.sharding import PartitionSpec as P

QBLOCK = 128
BETA_ONE = 0.9
BETA_TWO = 0.95
CORR_ONE = 1.0 - 0.9**10
CORR_TWO = 1.0 - 0.95**10
EPSILON = 1e-08
RATE = 0.002
BF = jnp.bfloat16
F32 = jnp.float32

MESH = pl.DeviceIdType.MESH
TILE = 16


class Spot:
    def __init__(self, n_ep, height):
        self.rep, self.ep = lax.axis_index("rep"), lax.axis_index("ep")
        self.core, self.y = self.rep % 2, self.rep // 2
        self.x, self.z = self.ep % 2, self.ep // 2
        self.n_ep, self.line, self.height = n_ep, n_ep // 2, height
        self.alone = height // TILE * 3 // 8 * TILE
        self.held = height - self.alone
        self.both = self.held - self.alone
        self.start = self.y * self.alone
        self.x_peer = (self.rep, self.z * 2 + 1 - self.x)
        self.y_peer = ((1 - self.y) * 2 + self.core, self.ep)
        self.core_peer = (self.y * 2 + 1 - self.core, self.ep)
        self.order = []
        for k in range(1, self.line // 2 + 1):
            self.order += [k] if k == self.line - k else [k, self.line - k]

    def near(self, j):
        last = self.line - 1
        few = jnp.where(2 * self.z < last, self.z, last - self.z)
        far = jnp.where(2 * self.z < last, 1, -1)
        sign = jnp.where(j < 2 * few, 1 - 2 * (j % 2), far)
        return self.z + sign * jnp.where(j < 2 * few, j // 2 + 1, j - few + 1), sign

    def z_peer(self, k):
        return (self.rep, (self.z + k) % self.line * 2 + self.x)

    def meet(self):
        barrier = pltpu.get_barrier_semaphore()
        peers = [self.z_peer(k) for k in range(1, self.line)]
        peers += [self.x_peer, self.y_peer, self.core_peer]
        for peer in peers:
            pl.semaphore_signal(barrier, inc=1, device_id=peer, device_id_type=MESH)
        pl.semaphore_wait(barrier, len(peers))


def tiled(value):
    return pl.multiple_of(value, TILE)


def remote(src, dst, send, recv, peer):
    return pltpu.make_async_remote_copy(
        src_ref=src, dst_ref=dst, send_sem=send, recv_sem=recv, device_id=peer, device_id_type=MESH
    )


class Gather:
    def __init__(self, at, own, out, sems):
        self.at, self.own, self.out = at, own, out
        (self.zs, self.xs, self.ys, self.c1s, self.c2s, self.r1, self.r2, self.r3, self.r4) = sems

    def part(self, half, ep, first, rows):
        return self.out.at[half, pl.ds(tiled(ep * self.at.height + first), rows)]

    def mine(self, ep):
        return self.part(self.at.core, ep, self.at.start, self.at.held)

    def first_copies(self, act):
        at = self.at
        src = self.own.at[at.core, pl.ds(tiled(at.start), at.held)]

        def to(sem, peer):
            return remote(src, self.mine(at.ep), sem, self.r1.at[at.ep], peer)

        @pl.when(at.z + 1 < at.line)
        def _():
            act(to(self.zs.at[at.line - 1], at.z_peer(1)))

        @pl.when(at.z > 0)
        def _():
            act(to(self.zs.at[at.line], at.z_peer(at.line - 1)))

        act(to(self.xs.at[at.line - 1], at.x_peer))

    def line_copies(self, j, act):
        at = self.at
        z, sign = at.near(j)
        ep = z * 2 + at.x
        rows = self.mine(ep)
        onward = at.z - sign

        @pl.when((onward >= 0) & (onward < at.line))
        def _():
            peer = (at.rep, onward * 2 + at.x)
            act(remote(rows, rows, self.zs.at[j], self.r1.at[ep], peer))

        act(remote(rows, rows, self.xs.at[j], self.r1.at[ep], at.x_peer))

    def share_copies(self, ep, act):
        at = self.at
        if at.alone:
            rows = self.part(at.core, ep, at.y * at.held, at.alone)
            act(remote(rows, rows, self.ys.at[ep], self.r2.at[ep], at.y_peer))
        act(remote(self.mine(ep), self.mine(ep), self.c1s.at[ep], self.r3.at[ep], at.core_peer))

    def late_copy(self, ep):
        at = self.at
        rows = self.part(at.core, ep, (1 - at.y) * at.held, at.alone)
        return remote(rows, rows, self.c2s.at[ep], self.r4.at[ep], at.core_peer)

    def arrive(self, dst, recv):
        remote(dst, dst, self.zs.at[0], recv, self.at.x_peer).wait_recv()

    def start(self):
        self.first_copies(lambda copy: copy.start())

    def from_line(self, j):
        at = self.at
        ep = at.near(j)[0] * 2 + at.x
        self.arrive(self.mine(ep), self.r1.at[ep])
        self.line_copies(j, lambda copy: copy.start())
        self.share_copies(ep, lambda copy: copy.start())
        return ep

    def from_pair(self, j):
        at = self.at
        ep = (at.z if j < 0 else at.near(j)[0]) * 2 + 1 - at.x
        self.arrive(self.mine(ep), self.r1.at[ep])
        self.share_copies(ep, lambda copy: copy.start())
        return ep

    def late(self, ep):
        at = self.at
        if at.alone:
            rows = self.part(at.core, ep, (1 - at.y) * at.held, at.alone)
            self.arrive(rows, self.r2.at[ep])
            self.late_copy(ep).start()

    def whole(self, ep):
        at = self.at
        self.arrive(self.part(1 - at.core, ep, at.start, at.held), self.r3.at[ep])
        if at.alone:
            rows = self.part(1 - at.core, ep, (1 - at.y) * at.held, at.alone)
            self.arrive(rows, self.r4.at[ep])

    def relay(self, tasks, use):
        at = self.at
        tasks = list(tasks)
        order = []
        for j in range(at.line - 1):
            for step, k in ((self.from_line, j), (self.from_pair, j - 1)):
                order.append(step(k))
                if tasks:
                    tasks.pop(0)()
        order.append(self.from_pair(at.line - 2))
        for task in tasks:
            task()
        behind = None
        for ep in order:
            self.late(ep)
            if behind is not None:
                self.whole(behind)
                use(behind)
            behind = ep
        self.whole(behind)
        use(behind)

    def end(self):
        at = self.at

        def done(copy):
            copy.wait_send()

        self.first_copies(done)
        for j in range(at.line - 1):
            self.line_copies(j, done)

        @pl.loop(1, at.n_ep)
        def _(k):
            ep = (at.ep + k) % at.n_ep
            self.share_copies(ep, done)
            if at.alone:
                self.late_copy(ep).wait_send()


def gather_sems(n_ep):
    line = n_ep // 2
    return [pltpu.SemaphoreType.DMA((line + 1,)), pltpu.SemaphoreType.DMA((line,))] + [
        pltpu.SemaphoreType.DMA((n_ep,)) for _ in range(7)
    ]


class Reduce:
    def __init__(self, at, term, fill, inp, out, bufs, sems):
        self.at, self.term, self.fill, self.inp, self.out = at, term, fill, inp, out
        (self.bc, self.s1, self.by, self.s2, self.bx, self.bz, self.fin, self.by2) = bufs
        (self.cs, self.cr, self.ys, self.yr, self.xs, self.xr, self.zs, self.zr, self.fs, self.fr) = sems

    def block(self, i):
        at = self.at
        far = jnp.where(i < at.line, 1, 0)
        z = (at.z + 1 + i) % at.line
        x = at.x + far - 2 * at.x * far
        return z, z * 2 + x

    def core_copy(self, ep):
        at = self.at
        return remote(
            self.inp.at[1 - at.core, pl.ds(tiled(ep * at.height), at.height)],
            self.bc.at[ep],
            self.cs.at[ep],
            self.cr.at[ep],
            at.core_peer,
        )

    def y_copy(self, ep):
        at = self.at
        return remote(
            self.s1.at[ep, pl.ds(tiled((1 - at.y) * at.held), at.alone)],
            self.by.at[ep],
            self.ys.at[ep],
            self.yr.at[ep],
            at.y_peer,
        )

    def x_copy(self, z, ep):
        return remote(self.s2.at[ep], self.bx.at[z], self.xs.at[z], self.xr.at[z], self.at.x_peer)

    def z_copy(self, k, ep):
        at = self.at
        return remote(self.s2.at[ep], self.bz.at[k], self.zs.at[k], self.zr.at[k], at.z_peer(k))

    def first(self, i):
        at = self.at
        _, ep = self.block(i)
        self.core_copy(ep).wait_recv()
        here = self.inp[at.core, pl.ds(tiled(ep * at.height), at.height)].astype(F32)
        self.s1[ep] = (here + self.bc[ep].astype(F32)).astype(BF)
        if at.alone:
            self.y_copy(ep).start()

    def pieces(self, ep):
        at = self.at
        found = []
        if at.alone:
            self.y_copy(ep).wait_recv()
            value = self.s1[ep, pl.ds(tiled(at.y * at.held), at.alone)].astype(F32)
            found.append((tiled(at.y * at.both), at.alone, value + self.by[ep].astype(F32)))
        value = self.s1[ep, pl.ds(at.alone, at.both)].astype(F32)
        found.append((tiled((1 - at.y) * at.alone), at.both, value))
        return found

    def second_far(self, i):
        z, ep = self.block(i)
        for first, rows, value in self.pieces(ep):
            self.s2[ep, pl.ds(first, rows)] = value.astype(BF)
        self.x_copy(z, ep).start()

    def second_near(self, i):
        z, ep = self.block(i)
        found = self.pieces(ep)
        self.x_copy(z, ep).wait_recv()
        for first, rows, value in found:
            total = value + self.bx[z, pl.ds(first, rows)].astype(F32)
            self.s2[ep, pl.ds(first, rows)] = total.astype(BF)

    def make(self, i):
        at = self.at
        _, ep = self.block(i)
        rows = pl.ds(tiled(ep * at.height), at.height)
        self.inp[1 - at.core, rows] = self.term(1 - at.core, rows).astype(BF)
        self.core_copy(ep).start()
        self.inp[at.core, rows] = self.term(at.core, rows).astype(BF)

    def ahead(self, i, lag):
        @pl.when(i + 2 * lag < self.at.n_ep)
        def _():
            self.make(i + 2 * lag)

        @pl.when(i + lag < self.at.n_ep)
        def _():
            self.first(i + lag)

    def run(self, lag=2):
        at = self.at
        self.make(0)
        for i in range(lag):
            for j in range(2 * i + 1, min(2 * i + 3, 2 * lag)):
                self.make(j)
            self.first(i)

        @pl.loop(0, at.line)
        def _(i):
            self.ahead(i, lag)
            self.second_far(i)
            self.fill(i)

        @pl.loop(at.line, at.n_ep - 1)
        def _(i):
            self.ahead(i, lag)
            self.second_near(i)
            k = i - at.line + 1
            _, ep = self.block(i)
            self.z_copy(k, ep).start()
            self.fill(i)

        self.second_near(at.n_ep - 1)
        self.fill(at.n_ep - 1)

    def finish(self):
        at = self.at
        total = self.s2[at.ep].astype(F32)
        for k in range(1, at.line):
            self.z_copy(k, at.ep).wait_recv()
            total += self.bz[k].astype(F32)
        self.fin[...] = total.astype(BF)
        swap = remote(self.fin, self.by2, self.fs.at[0], self.fr.at[0], at.y_peer)
        swap.start()
        half = self.out.at[at.core]
        if at.alone:
            half[pl.ds(tiled(at.y * at.held), at.alone)] = self.fin[
                pl.ds(tiled(at.y * at.both), at.alone)
            ]
        swap.wait()
        if at.alone:
            half[pl.ds(tiled((1 - at.y) * at.held), at.alone)] = self.by2[
                pl.ds(tiled((1 - at.y) * at.both), at.alone)
            ]
        here = self.fin[pl.ds(tiled((1 - at.y) * at.alone), at.both)].astype(F32)
        there = self.by2[pl.ds(tiled(at.y * at.alone), at.both)].astype(F32)
        half[pl.ds(at.alone, at.both)] = (here + there).astype(BF)
        last = remote(half, half, self.fs.at[1], self.fr.at[1], at.core_peer)
        last.start()
        last.wait_send()
        other = self.out.at[1 - at.core]
        remote(other, other, self.fs.at[1], self.fr.at[1], at.core_peer).wait_recv()

        @pl.loop(0, at.n_ep)
        def _(i):
            _, ep = self.block(i)
            self.core_copy(ep).wait_send()
            if at.alone:
                self.y_copy(ep).wait_send()

        @pl.loop(0, at.line)
        def _(i):
            z, ep = self.block(i)
            self.x_copy(z, ep).wait_send()

        @pl.loop(1, at.line)
        def _(k):
            self.z_copy(k, at.ep).wait_send()


def reduce_bufs(n_ep, height, feature):
    line = n_ep // 2
    alone = height // TILE * 3 // 8 * TILE
    held = height - alone
    shapes = [
        (n_ep, height),
        (n_ep, height),
        (n_ep, max(alone, TILE)),
        (n_ep, held),
        (line, held),
        (line, held),
        (held,),
        (held,),
    ]
    counts = [n_ep, n_ep, n_ep, n_ep, line, line, line, line, 2, 2]
    return [pltpu.VMEM(s + (feature,), BF) for s in shapes] + [
        pltpu.SemaphoreType.DMA((c,)) for c in counts
    ]


CHUNK = 256
LANES = 128


def dot(a, b, dims=((1,), (0,))):
    return lax.dot_general(a, b, (dims, ((), ())), preferred_element_type=F32)


def step_kernel(n_ep, total_rows, *refs):
    sources = refs[:8]
    (token_grad, step_dir, new_weight, next_gate) = refs[8:12]
    (pick, pick_t, tok_t, spread, acc, dgate, whole, again, inp, grad, own, own_b) = refs[12:24]
    bufs, sems = refs[24:32], refs[32:42]
    sems_one, sems_two, scales = refs[42:51], refs[51:60], refs[60]
    (tokens, route, cot, weight, fq, fs, sq, ss) = refs[61:69]
    landed = refs[69]
    halves, height, feature = weight.shape
    count, width = tokens.shape
    picked = route.shape[1]
    at = Spot(n_ep, height)
    by_block = height % LANES == 0

    def tiles(extent, body):
        size = CHUNK if extent % CHUNK == 0 else extent

        @pl.loop(0, extent // size)
        def _(t):
            body(pl.ds(pl.multiple_of(t * size, size), size))

    def project(half, cols, matrix, brows, fresh):
        def body(rows):
            value = dot(tokens[rows, cols], matrix[half, brows])
            acc[half, rows] = value if fresh else acc[half, rows] + value

        tiles(count, body)

    def use_block(matrix, ep, fresh=False):
        if by_block:
            spot = pl.ds(pl.multiple_of(ep * height, height), height)
            for half in range(halves):
                project(half, spot, matrix, spot, fresh)

    def use_rest(matrix):
        if not by_block:
            for half in range(halves):
                for j in range(width // CHUNK):
                    spot = pl.ds(j * CHUNK, CHUNK)
                    project(half, spot, matrix, spot, j == 0)

    def scatter(half):
        def body(rows):
            spots = lax.broadcasted_iota(jnp.int32, (rows.size, picked), 0) + rows.start
            hits = (spots == route[pl.ds(half, 1), :]).astype(F32).astype(BF)
            pick[half, rows] = hits
            spread[half, rows] = dot(hits, cot[half]).astype(BF)

        tiles(count, body)

    def flip_pick(half):
        pick_t[half] = pick[half].T

    def flip(j):
        spot = pl.ds(j * CHUNK, CHUNK)
        tok_t[spot, :] = tokens[:, spot].T

    def both(task, *args):
        for half in range(halves):
            task(half)

    own_rows = pl.ds(tiled(at.ep * height), height)
    one = Gather(at, own, whole, sems_one)
    loads = [
        pltpu.make_async_copy(src, dst, landed.at[i])
        for i, (src, dst) in enumerate(zip(sources, refs[61:69]))
    ]
    for i in (3, 1, 2, 0, 4, 5, 6, 7):
        loads[i].start()
    loads[3].wait()
    own[...] = weight[...].astype(BF)
    at.meet()
    one.start()
    whole[:, own_rows] = own[...]
    for i in (1, 2, 0):
        loads[i].wait()
    flips = [functools.partial(flip, j) for j in range(width // CHUNK)]
    tasks = [functools.partial(scatter, h) for h in range(halves)]
    tasks.insert(1, lambda: use_block(whole, at.ep, True))
    tasks += [functools.partial(flip_pick, h) for h in range(halves)]
    while flips:
        pair = flips[:4]
        flips = flips[4:]
        tasks.append(lambda pair=pair: [f() for f in pair])
    one.relay(tasks, lambda ep: use_block(whole, ep))
    use_rest(whole)

    for half in range(halves):

        def shape_grad(rows):
            gate = acc[half, rows]
            sig = 1.0 / (1.0 + jnp.exp(-gate))
            value = spread[half, rows].astype(F32) * sig * (1.0 + gate * (1.0 - sig))
            dgate[half, rows] = value.astype(BF)

        tiles(count, shape_grad)

    def term(half, rows):
        return dot(tok_t[rows, :], dgate[half])

    def back(j):
        @pl.when(j < width // CHUNK)
        def _():
            spot = pl.ds(pl.multiple_of(j * CHUNK, CHUNK), CHUNK)

            def body(rows):
                value = dot(dgate[0, rows], whole[0, spot], ((1,), (1,)))
                for half in range(1, halves):
                    value += dot(dgate[half, rows], whole[half, spot], ((1,), (1,)))
                token_grad[rows, spot] = value.astype(BF)

            tiles(count, body)

    job = Reduce(at, term, back, inp, grad, bufs, sems)
    job.run()
    for j in range(n_ep, width // CHUNK):
        back(j)
    job.finish()

    for i in (4, 5, 6, 7):
        loads[i].wait()
    slab = 64 if height % 64 == 0 else height
    for half in range(halves):
        scales[0] = fs[half].T
        scales[1] = ss[half].T

        @pl.loop(0, height // slab)
        def _(t):
            rows = pl.ds(pl.multiple_of(t * slab, slab), slab)
            for q in range(feature // QBLOCK):
                cols = pl.ds(q * QBLOCK, QBLOCK)
                here = (half, rows, cols)
                g = grad[here].astype(F32) / total_rows
                first = BETA_ONE * (fq[here].astype(F32) * scales[0, rows, pl.ds(q, 1)])
                second = BETA_TWO * (sq[here].astype(F32) * scales[1, rows, pl.ds(q, 1)])
                first += (1.0 - BETA_ONE) * g
                second += (1.0 - BETA_TWO) * g * g
                step = first / CORR_ONE / (jnp.sqrt(second / CORR_TWO) + EPSILON)
                fresh = weight[here] - RATE * step
                step_dir[here] = step
                new_weight[here] = fresh
                own_b[here] = fresh.astype(BF)

    two = Gather(at, own_b, again, sems_two)
    two.start()
    again[:, own_rows] = own_b[...]
    two.relay([lambda: use_block(again, at.ep, True)], lambda ep: use_block(again, ep))
    use_rest(again)
    for half in range(halves):
        rounded = acc[half].astype(BF)

        def put(rows):
            next_gate[half, rows] = dot(pick_t[half, rows], rounded).astype(BF)

        tiles(picked, put)
    one.end()
    two.end()


def on_device(tokens, route, cotangent, weight, first_q, first_scale, second_q, second_scale):
    n_rep = lax.axis_size("rep")
    n_ep = lax.axis_size("ep")
    halves, picked = route.shape
    count, width = tokens.shape
    feature = cotangent.shape[2]
    height = weight.shape[1]
    total_rows = picked * n_rep * n_ep
    vmem = pltpu.VMEM
    scratch = [
        vmem((halves, count, picked), BF),
        vmem((halves, picked, count), BF),
        vmem((width, count), BF),
        vmem((halves, count, feature), BF),
        vmem((halves, count, feature), F32),
        vmem((halves, count, feature), BF),
        vmem((halves, width, feature), BF),
        vmem((halves, width, feature), BF),
        vmem((halves, width, feature), BF),
        vmem((halves, height, feature), BF),
        vmem((halves, height, feature), BF),
        vmem((halves, height, feature), BF),
    ]
    scratch += reduce_bufs(n_ep, height, feature) + gather_sems(n_ep) + gather_sems(n_ep)
    scratch += [vmem((2, height, first_scale.shape[2]), F32)]
    given = [tokens, route, cotangent, weight, first_q]
    given += [first_scale.transpose(0, 2, 1), second_q, second_scale.transpose(0, 2, 1)]
    given = [pltpu.with_memory_space_constraint(a, pltpu.HBM) for a in given]
    scratch += [vmem(a.shape, a.dtype) for a in given] + [pltpu.SemaphoreType.DMA((8,))]
    in_vmem = pl.BlockSpec(memory_space=pltpu.VMEM)
    return pl.pallas_call(
        functools.partial(step_kernel, n_ep, total_rows),
        out_shape=(
            jax.ShapeDtypeStruct(tokens.shape, BF),
            jax.ShapeDtypeStruct(weight.shape, F32),
            jax.ShapeDtypeStruct(weight.shape, F32),
            jax.ShapeDtypeStruct(cotangent.shape, BF),
        ),
        in_specs=[pl.BlockSpec(memory_space=pltpu.HBM)] * 8,
        out_specs=(in_vmem,) * 4,
        scratch_shapes=scratch,
        compiler_params=pltpu.CompilerParams(
            collective_id=1, has_side_effects=True, vmem_limit_bytes=46 << 20
        ),
        name="hot_step",
    )(*given)


def solution(mesh):
    in_specs = (
        P(("rep", "ep"), None),
        P(None, ("rep", "ep")),
        P(None, ("rep", "ep"), None),
        P(None, "ep", None),
        P(None, "ep", None),
        P(None, "ep", None),
        P(None, "ep", None),
        P(None, "ep", None),
    )
    out_specs = (
        P(("rep", "ep"), None),
        P(None, "ep", None),
        P(None, "ep", None),
        P(None, ("rep", "ep"), None),
    )
    return jax.shard_map(
        on_device, mesh=mesh, in_specs=in_specs, out_specs=out_specs, check_vma=False
    )
```
